32 devices in a mesh: cg: 8 (over z, x), vg: 4 (over y, core).
Axes of the slice: x: 2, y: 2, z: 4, core: 2. Of those that a mesh axis runs over, the one named last changes fastest.
Arguments:
- con_embed: float32 [32768, 128], P(('cg', 'vg')), may hold values from -6 to 6
- var_embed: float32 [32768, 128], P(('vg', 'cg')), may hold values from -6 to 6
- row_coef: float32 [32768], P(('cg', 'vg')), may hold values from 0.3 to 3
- col_coef: float32 [32768], P(('vg', 'cg')), may hold values from 0.3 to 3
- self_weight: float32 [128, 128], replicated, may hold values from -0.5 to 0.5
- msg_weight: float32 [128, 128], replicated, may hold values from -0.0234375 to 0.0234375
- timestep: int32 [1], replicated, may hold values from 0 to 999
- tile_rows: int32 [8, 4, 16], P('cg', 'vg'), may hold values from 0 to 7, as said below
- tile_cols: int32 [8, 4, 16], P('cg', 'vg'), may hold values from 0 to 15, as said below
- pattern: bfloat16 [8, 4, 16, 512, 512], P('cg', 'vg'), may hold values from -6 to 6
- cotangent: float32 [32768, 128], P(('cg', 'vg')), may hold values from -6 to 6
Outputs:
- con_update: float32 [32768, 128], P(('cg', 'vg'))
- grad_con: float32 [32768, 128], P(('cg', 'vg'))
- grad_var: float32 [32768, 128], P(('vg', 'cg'))
- grad_msg: float32 [128, 128], replicated
- grad_self: float32 [128, 128], replicated
The draws below stay inside these ranges and needn't reach their ends.
Inputs may be any that keep to these rules, and one draw needn't show every extreme that they name: `tile_rows`: every device lists tile row 0 and tile row 7; a device lists distinct tiles unless 16 exceeds 8 * 16, and repeated tiles add. `tile_cols`: every device lists tile column 0 and tile column 15, together with the rows above: tiles (0, 0) and (7, 15) are on every list.
All inputs are finite; a program needn't handle non-finite values.
Results may differ from the reference program's by a relative error of at most 0.007.
Values may be sent and summed in bfloat16 or wider, within the bound.
A program may use at most 128 MiB of HBM per device.

```python
import math
import jax
import jax.numpy as jnp
from jax import lax

H = 128
TB = 512
C_DEV = 1024
V_DEV = 1024
TILES = 16
NC = 32768
NV = 32768
RBLK = 8
CBLK = 16
N_CG = 8
N_VG = 4


def tile_pairs(key):
    block_total = RBLK * CBLK

    def single(subkey):
        perm_key, roll_key = jax.random.split(subkey)
        middle = jax.random.permutation(perm_key, block_total - 2) + 1
        listing = jnp.concatenate([jnp.array([block_total - 1, 0], dtype=jnp.int32), middle.astype(jnp.int32)])
        chosen = listing[jnp.arange(TILES, dtype=jnp.int32) % block_total]
        offset = jax.random.randint(roll_key, (), 0, TILES)
        return jnp.roll(chosen, offset)
    subkeys = jax.random.split(jax.random.fold_in(key, 11), N_CG * N_VG)
    chosen = jax.vmap(single)(subkeys).reshape(N_CG, N_VG, TILES)
    return (chosen // CBLK, chosen % CBLK)


def draw_tile_rows(key, part):
    return tile_pairs(key)[0]


def draw_tile_cols(key, part):
    return tile_pairs(key)[1]


def steps_of(stream_key, shape, pieces, low, high):
    def one(axis_at, blocks):
        heights = jax.random.uniform(jax.random.fold_in(jax.random.fold_in(stream_key, 6), axis_at), (blocks,), jnp.float32, low / len(pieces), high / len(pieces))
        return jnp.repeat(jnp.exp(heights), shape[axis_at] // blocks).reshape((-1,) + (1,) * (len(shape) - axis_at - 1))

    level = one(*pieces[0])
    for cut in pieces[1:]:
        level = level * one(*cut)
    return level


def gaussian(key, dims, width, most, cuts=(), kind=jnp.bfloat16):
    values = jax.random.normal(key, dims, jnp.float32) * width
    if len(cuts) > 0:
        values = steps_of(key, dims, cuts, -0.22, 0.18) * values
    return jnp.clip(values, min=-most, max=most).astype(kind)


def setup_inputs(seed: int = 0) -> dict:
    key_of = jax.random.split(jax.random.key(seed), 12)
    con_embed = gaussian(key_of[0], (NC, H), 1.0, 6.0, ((0, 32),), jnp.float32)
    var_embed = gaussian(key_of[1], (NV, H), 1.0, 6.0, ((0, 32),), jnp.float32)
    row_coef = jnp.clip(jnp.exp(math.log(3.0) - 2.3025851 * jax.random.uniform(key_of[2], (NC,), jnp.float32) ** steps_of(key_of[2], (NC,), ((0, 32),), -0.2, 0.2)), 0.3, 3.0)
    col_coef = jnp.clip(jnp.exp(math.log(3.0) - 2.3025851 * jax.random.uniform(key_of[3], (NV,), jnp.float32) ** steps_of(key_of[3], (NV,), ((0, 32),), -0.2, 0.2)), 0.3, 3.0)
    self_weight = gaussian(key_of[4], (H, H), H ** -0.5, 0.5, (), jnp.float32)
    msg_weight = gaussian(key_of[5], (H, H), (H * TB) ** -0.5, 0.0234375, (), jnp.float32)
    timestep = jax.random.randint(key_of[6], (1,), 0, 1000).astype(jnp.int32)
    tile_rows = draw_tile_rows(jax.random.fold_in(key_of[11], 71), 0)
    tile_cols = draw_tile_cols(jax.random.fold_in(key_of[11], 71), 0)
    pattern = gaussian(key_of[9], (N_CG, N_VG, TILES, TB, TB), 1.0, 6.0, ((0, 8), (1, 4)))
    cotangent = gaussian(key_of[10], (NC, H), 1.0, 6.0, ((0, 32),), jnp.float32)
    return dict(con_embed=con_embed, var_embed=var_embed, row_coef=row_coef, col_coef=col_coef, self_weight=self_weight, msg_weight=msg_weight, timestep=timestep, tile_rows=tile_rows, tile_cols=tile_cols, pattern=pattern, cotangent=cotangent)


def reference(con_embed, var_embed, row_coef, col_coef, self_weight, msg_weight, timestep, tile_rows, tile_cols, pattern, cotangent):
    highest = lax.Precision.HIGHEST
    group_rows = C_DEV * N_VG
    group_cols = V_DEV * N_CG
    row_list = tile_rows.reshape(-1, TILES)
    col_list = tile_cols.reshape(-1, TILES)
    pattern_list = pattern.reshape(-1, TILES, TB, TB)
    devices = jnp.arange(N_CG * N_VG, dtype=jnp.int32)
    projected = (jnp.dot(var_embed, msg_weight, precision=highest, preferred_element_type=jnp.float32) * col_coef[:, None]).astype(jnp.bfloat16)

    def forward(running, device):
        con_group = device // N_VG
        var_group = device % N_VG
        source = lax.dynamic_slice_in_dim(projected, (var_group * group_cols).astype(jnp.int32), group_cols, 0)
        source = source.reshape(CBLK, TB, H).astype(jnp.float32)
        tile_mask = pattern_list[device].astype(jnp.float32)
        products = jnp.einsum('trc,tch->trh', tile_mask, source[col_list[device]], precision=highest)
        selector = (row_list[device][None, :] == jnp.arange(RBLK, dtype=jnp.int32)[:, None]).astype(jnp.float32)
        partial_value = jnp.einsum('bt,trh->brh', selector, products, precision=highest).reshape(group_rows, H)
        offset = (con_group * group_rows).astype(jnp.int32)
        current = lax.dynamic_slice_in_dim(running, offset, group_rows, 0)
        return lax.dynamic_update_slice_in_dim(running, current + partial_value, offset, 0), None

    messages, _ = lax.scan(forward, jnp.zeros((NC, H), jnp.float32), devices)
    frequency = jnp.exp(-math.log(10000.0) * jnp.arange(H // 2, dtype=jnp.float32) / (H // 2))
    phases = timestep[0].astype(jnp.float32) * frequency
    time_embed = jnp.concatenate([jnp.sin(phases), jnp.cos(phases)])
    preact = jnp.dot(con_embed, self_weight, precision=highest, preferred_element_type=jnp.float32) + row_coef[:, None] * messages + time_embed[None, :]
    sigmoid_z = jax.nn.sigmoid(preact)
    con_update = con_embed + preact * sigmoid_z
    grad_pre = cotangent * sigmoid_z * (1.0 + preact * (1.0 - sigmoid_z))
    grad_con = cotangent + jnp.dot(grad_pre, self_weight.T, precision=highest, preferred_element_type=jnp.float32)
    grad_self = jnp.dot(con_embed.T, grad_pre, precision=highest, preferred_element_type=jnp.float32)
    grad_messages = (row_coef[:, None] * grad_pre).astype(jnp.bfloat16)

    def backward(running, device):
        con_group = device // N_VG
        var_group = device % N_VG
        source = lax.dynamic_slice_in_dim(grad_messages, (con_group * group_rows).astype(jnp.int32), group_rows, 0)
        source = source.reshape(RBLK, TB, H).astype(jnp.float32)
        tile_mask = pattern_list[device].astype(jnp.float32)
        products = jnp.einsum('trc,trh->tch', tile_mask, source[row_list[device]], precision=highest)
        selector = (col_list[device][None, :] == jnp.arange(CBLK, dtype=jnp.int32)[:, None]).astype(jnp.float32)
        partial_value = jnp.einsum('bt,tch->bch', selector, products, precision=highest).reshape(group_cols, H)
        offset = (var_group * group_cols).astype(jnp.int32)
        current = lax.dynamic_slice_in_dim(running, offset, group_cols, 0)
        return lax.dynamic_update_slice_in_dim(running, current + partial_value, offset, 0), None

    grad_projected, _ = lax.scan(backward, jnp.zeros((NV, H), jnp.float32), devices)
    grad_lin = col_coef[:, None] * grad_projected
    grad_var = jnp.dot(grad_lin, msg_weight.T, precision=highest, preferred_element_type=jnp.float32)
    grad_msg = jnp.dot(var_embed.T, grad_lin, precision=highest, preferred_element_type=jnp.float32)
    return (con_update, grad_con, grad_var, grad_msg, grad_self)
```

```python
import functools
import math

import jax
import jax.numpy as jnp
from jax import lax
from jax.experimental import pallas as pl
from jax.experimental.pallas import tpu as pltpu
from jax.sharding import PartitionSpec as P

H = 128
TB = 512
CHUNKS = 4
MESH = pl.DeviceIdType.MESH
HIGHEST = lax.Precision.HIGHEST
F32 = jnp.float32
BF16 = jnp.bfloat16


def rcopy(src, dst, send_sem, recv_sem, device):
    return pltpu.make_async_remote_copy(
        src_ref=src, dst_ref=dst, send_sem=send_sem, recv_sem=recv_sem,
        device_id=device, device_id_type=MESH,
    )


def rows(index, size):
    return pl.ds(pl.multiple_of(index * size, size), size)


def dot(a, b, dims=((1,), (0,))):
    return lax.dot_general(a, b, (dims, ((), ())), precision=HIGHEST, preferred_element_type=F32)


def column(coef_ref, out_ref):
    for i in range(coef_ref.shape[0]):
        out_ref[pl.ds(i * H, H), :] = jnp.broadcast_to(coef_ref[pl.ds(i, 1), :], (H, H)).T


def gather_kernel(n_cg, var_ref, weight_ref, coef_ref, out_ref, coef, send, recv_z, recv_x):
    n_z = n_cg // 2
    cg, vg = lax.axis_index("cg"), lax.axis_index("vg")
    z, x = cg // 2, cg % 2
    size = var_ref.shape[0]
    barrier = pltpu.get_barrier_semaphore()
    pl.semaphore_signal(barrier, inc=1, device_id=(z * 2 + 1 - x, vg), device_id_type=MESH)
    for s in (1, -1):
        @pl.when((z + s >= 0) & (z + s < n_z))
        def _():
            pl.semaphore_signal(barrier, inc=1, device_id=((z + s) * 2 + x, vg), device_id_type=MESH)

    column(coef_ref, coef)
    out_ref[rows(cg, size), :] = (dot(var_ref[...], weight_ref[...]) * coef[...]).astype(BF16)
    lines = jnp.where(z > 0, 1, 0) + jnp.where(z < n_z - 1, 1, 0)
    pl.semaphore_wait(barrier, 1 + lines)

    def z_copy(zs, way):
        block = out_ref.at[rows(zs * 2 + x, size), :]
        step = 1 if way == 0 else -1
        return rcopy(block, block, send.at[way, zs], recv_z.at[zs], ((z + step) * 2 + x, vg))

    def x_copy(zs):
        block = out_ref.at[rows(zs * 2 + x, size), :]
        return rcopy(block, block, send.at[2, zs], recv_x.at[zs], (z * 2 + 1 - x, vg))

    def x_wait(zs):
        block = out_ref.at[rows(zs * 2 + 1 - x, size), :]
        rcopy(block, block, send.at[2, zs], recv_x.at[zs], (z * 2 + 1 - x, vg)).wait_recv()

    def on(zs, way, act):
        if way == 0:
            pl.when((zs >= 0) & (zs <= z) & (z + 1 < n_z))(act)
        else:
            pl.when((zs < n_z) & (zs >= z) & (z >= 1))(act)

    for way in (0, 1):
        on(z, way, lambda way=way: z_copy(z, way).start())
    x_copy(z).start()
    for d in range(1, n_z):
        for way in (0, 1):
            zs = z - d if way == 0 else z + d

            @pl.when((zs >= 0) & (zs < n_z))
            def _(zs=zs, way=way):
                z_copy(zs, way).wait_recv()
                on(zs, way, lambda: z_copy(zs, way).start())
                x_copy(zs).start()

    for zs in range(n_z):
        x_wait(zs)
        x_copy(zs).wait_send()
    for d in range(n_z):
        for way in (0, 1):
            zs = z - d if way == 0 else z + d
            on(zs, way, lambda zs=zs, way=way: z_copy(zs, way).wait_send())


def gather_projected(var_embed, msg_weight, col_coef, n_cg):
    size = var_embed.shape[0]
    vmem = pl.BlockSpec(memory_space=pltpu.VMEM)
    return pl.pallas_call(
        functools.partial(gather_kernel, n_cg),
        name="gather_projected",
        out_shape=jax.ShapeDtypeStruct((n_cg * size, H), BF16),
        in_specs=[vmem] * 3,
        out_specs=vmem,
        scratch_shapes=[
            pltpu.VMEM((size, H), F32),
            pltpu.SemaphoreType.DMA((3, n_cg // 2)),
            pltpu.SemaphoreType.DMA((n_cg // 2,)),
            pltpu.SemaphoreType.DMA((n_cg // 2,)),
        ],
        compiler_params=pltpu.CompilerParams(collective_id=0, has_side_effects=True),
    )(var_embed, msg_weight, col_coef.reshape(-1, H))


def tile_kernel(per, transposed, to_ref, from_ref, pattern_ref, source_ref, out_ref):
    step = pl.program_id(0)

    @pl.when(step == 0)
    def _():
        out_ref[...] = jnp.zeros_like(out_ref)

    for t in range(per):
        k = step * per + t
        source = source_ref[rows(from_ref[k], TB), :]
        dims = ((0,), (0,)) if transposed else ((1,), (0,))
        target = rows(to_ref[k], TB)
        out_ref[target, :] += lax.dot_general(
            pattern_ref[t], source, (dims, ((), ())), preferred_element_type=F32
        )


def tile_sum(to_index, from_index, patterns, source, out_rows, transposed):
    count = patterns.shape[0]
    per = math.gcd(count, 4)
    return pl.pallas_call(
        functools.partial(tile_kernel, per, transposed),
        name="tiles_back" if transposed else "tiles_forward",
        out_shape=jax.ShapeDtypeStruct((out_rows, H), F32),
        grid_spec=pltpu.PrefetchScalarGridSpec(
            num_scalar_prefetch=2,
            grid=(count // per,),
            in_specs=[
                pl.BlockSpec((per, TB, TB), lambda i, *_: (i, 0, 0)),
                pl.BlockSpec(source.shape, lambda i, *_: (0, 0)),
            ],
            out_specs=pl.BlockSpec((out_rows, H), lambda i, *_: (0, 0)),
        ),
        compiler_params=pltpu.CompilerParams(dimension_semantics=("arbitrary",)),
    )(to_index, from_index, patterns, source)


def middle_kernel(
    n_vg, part_ref, con_ref, cot_ref, weight_ref, coef_ref, time_ref,
    update_ref, grad_con_ref, self_ref, whole_ref,
    coef, pre, from_core, to_peer, from_peer,
    core_send, core_recv, peer_send, peer_recv, own_send, pass_send, block_recv, pair_recv,
):
    n_hi = n_vg // 2
    cg, vg = lax.axis_index("cg"), lax.axis_index("vg")
    hi, core = vg // 2, vg % 2
    pair = (cg, hi * 2 + 1 - core)
    size = con_ref.shape[0]
    piece = size // CHUNKS
    barrier = pltpu.get_barrier_semaphore()
    pl.semaphore_signal(barrier, inc=1, device_id=pair, device_id_type=MESH)
    ups = [lax.rem(hi + j, n_hi) for j in range(n_hi)]
    downs = [lax.rem(hi + n_hi - j, n_hi) for j in range(n_hi)]
    for j in range(1, n_hi):
        pl.semaphore_signal(barrier, inc=1, device_id=(cg, ups[j] * 2 + core), device_id_type=MESH)
    pl.semaphore_wait(barrier, n_hi)

    def cut(block, k):
        return rows(block * CHUNKS + k, piece)

    def core_copy(h, k):
        return rcopy(
            part_ref.at[cut(h * 2 + 1 - core, k), :], from_core.at[cut(h, k), :],
            core_send.at[h, k], core_recv.at[h, k], pair,
        )

    def peer_copy(j, k):
        return rcopy(
            to_peer.at[cut(j - 1, k), :], from_peer.at[cut(j - 1, k), :],
            peer_send.at[j - 1, k], peer_recv.at[j - 1, k], (cg, ups[j] * 2 + core),
        )

    def own_copy(j, k):
        block = whole_ref.at[cut(vg, k), :]
        return rcopy(block, block, own_send.at[j - 1, k], block_recv.at[j - 1, k], (cg, ups[j] * 2 + core))

    def block_wait(j, k):
        block = whole_ref.at[cut(downs[j] * 2 + core, k), :]
        rcopy(block, block, own_send.at[j - 1, k], block_recv.at[j - 1, k], pair).wait_recv()

    def pass_copy(h, k):
        block = whole_ref.at[cut(h * 2 + core, k), :]
        return rcopy(block, block, pass_send.at[h, k], pair_recv.at[h, k], pair)

    def pass_wait(h, k):
        block = whole_ref.at[cut(h * 2 + 1 - core, k), :]
        rcopy(block, block, pass_send.at[h, k], pair_recv.at[h, k], pair).wait_recv()

    for j in list(range(1, n_hi)) + [0]:
        for k in range(CHUNKS):
            core_copy(ups[j], k).start()
    for j in range(1, n_hi):
        for k in range(CHUNKS):
            core_copy(ups[j], k).wait_recv()
            to_peer[cut(j - 1, k), :] = (
                part_ref[cut(ups[j] * 2 + core, k), :] + from_core[cut(ups[j], k), :]
            ).astype(BF16)
            peer_copy(j, k).start()
    column(coef_ref, coef)
    pre[...] = dot(con_ref[...], weight_ref[...]) + time_ref[...]
    for k in range(CHUNKS):
        core_copy(hi, k).wait_recv()
        here = pl.ds(k * piece, piece)
        messages = part_ref[cut(vg, k), :] + from_core[cut(hi, k), :]
        for j in range(1, n_hi):
            peer_copy(j, k).wait_recv()
            messages = messages + from_peer[cut(j - 1, k), :].astype(F32)
        preact = pre[here, :] + coef[here, :] * messages
        sig = jax.nn.sigmoid(preact)
        update_ref[here, :] = con_ref[here, :] + preact * sig
        grad_pre = cot_ref[here, :] * sig * (1.0 + preact * (1.0 - sig))
        pre[here, :] = grad_pre
        whole_ref[cut(vg, k), :] = (coef[here, :] * grad_pre).astype(BF16)
        for j in range(1, n_hi):
            own_copy(j, k).start()
        pass_copy(hi, k).start()
    grad_con_ref[...] = cot_ref[...] + dot(pre[...], weight_ref[...], ((1,), (1,)))
    self_ref[...] = dot(con_ref[...], pre[...], ((0,), (0,)))
    for k in range(CHUNKS):
        for j in range(1, n_hi):
            block_wait(j, k)
            pass_copy(downs[j], k).start()
    for h in range(n_hi):
        for k in range(CHUNKS):
            pass_wait(h, k)
            pass_copy(h, k).wait_send()
            core_copy(h, k).wait_send()
    for j in range(1, n_hi):
        for k in range(CHUNKS):
            peer_copy(j, k).wait_send()
            own_copy(j, k).wait_send()


def middle(part, con_embed, cotangent, self_weight, row_coef, time_embed, n_vg):
    size = con_embed.shape[0]
    n_hi = n_vg // 2
    vmem = pl.BlockSpec(memory_space=pltpu.VMEM)
    full = jax.ShapeDtypeStruct((size, H), F32)
    others = max(n_hi - 1, 1)
    dma = lambda n: pltpu.SemaphoreType.DMA((n, CHUNKS))
    return pl.pallas_call(
        functools.partial(middle_kernel, n_vg),
        name="middle",
        out_shape=(
            full, full, jax.ShapeDtypeStruct((H, H), F32),
            jax.ShapeDtypeStruct((n_vg * size, H), BF16),
        ),
        in_specs=[vmem] * 6,
        out_specs=(vmem,) * 4,
        scratch_shapes=[
            pltpu.VMEM((size, H), F32),
            pltpu.VMEM((size, H), F32),
            pltpu.VMEM((n_hi * size, H), F32),
            pltpu.VMEM((others * size, H), BF16),
            pltpu.VMEM((others * size, H), BF16),
            dma(n_hi), dma(n_hi), dma(others), dma(others),
            dma(others), dma(n_hi), dma(others), dma(n_hi),
        ],
        compiler_params=pltpu.CompilerParams(collective_id=1, has_side_effects=True),
    )(part, con_embed, cotangent, self_weight, row_coef.reshape(-1, H), time_embed.reshape(1, H))


class Total:
    def __init__(self, n_cg, n_vg, local, out, cuts, quarters, sem):
        self.n_cg, self.n_vg = n_cg, n_vg
        self.local, self.out, self.cuts, self.quarters, self.sem = local, out, cuts, quarters, sem
        self.cg, self.vg = lax.axis_index("cg"), lax.axis_index("vg")
        self.size = H // n_vg

    def a(self, j):
        v = lax.rem(self.vg + j, self.n_vg)
        return rcopy(
            self.local.at[rows(v, self.size), :], self.cuts.at[j - 1],
            self.sem.at[0, j], self.sem.at[1, j], (self.cg, v),
        )

    def b(self, j):
        c = lax.rem(self.cg + j, self.n_cg)
        block = self.quarters.at[self.cg]
        return rcopy(block, block, self.sem.at[2, j], self.sem.at[3, j], (c, self.vg))

    def b_wait(self, j):
        c = lax.rem(self.cg + self.n_cg - j, self.n_cg)
        block = self.quarters.at[c]
        rcopy(block, block, self.sem.at[2, j], self.sem.at[3, j], (c, self.vg)).wait_recv()

    def c(self, j):
        v = lax.rem(self.vg + j, self.n_vg)
        block = self.out.at[rows(self.vg, self.size), :]
        return rcopy(block, block, self.sem.at[4, j], self.sem.at[5, j], (self.cg, v))

    def c_wait(self, j):
        v = lax.rem(self.vg + self.n_vg - j, self.n_vg)
        block = self.out.at[rows(v, self.size), :]
        rcopy(block, block, self.sem.at[4, j], self.sem.at[5, j], (self.cg, v)).wait_recv()

    def start(self):
        for j in range(1, self.n_vg):
            self.a(j).start()

    def second(self):
        value = self.local[rows(self.vg, self.size), :]
        for j in range(1, self.n_vg):
            self.a(j).wait_recv()
            value = value + self.cuts[j - 1]
        self.quarters[self.cg] = value
        for j in range(1, self.n_cg):
            self.b(j).start()

    def third(self):
        for j in range(1, self.n_cg):
            self.b_wait(j)
            self.b(j).wait_send()
        value = self.quarters[0]
        for c in range(1, self.n_cg):
            value = value + self.quarters[c]
        self.out[rows(self.vg, self.size), :] = value
        for j in range(1, self.n_vg):
            self.c(j).start()

    def finish(self):
        for j in range(1, self.n_vg):
            self.c_wait(j)
            self.c(j).wait_send()
            self.a(j).wait_send()


def last_kernel(
    n_cg, n_vg, part_ref, var_ref, weight_ref, coef_ref, self_ref,
    grad_var_ref, grad_msg_ref, grad_self_ref,
    coef, to_x, from_x, to_z, from_z, local_msg,
    cuts_a, cuts_b, quarters_a, quarters_b, x_send, x_recv, z_send, z_recv, sem_a, sem_b,
):
    n_z = n_cg // 2
    cg, vg = lax.axis_index("cg"), lax.axis_index("vg")
    z, x = cg // 2, cg % 2
    size = var_ref.shape[0]
    barrier = pltpu.get_barrier_semaphore()
    for j in range(1, n_cg):
        pl.semaphore_signal(barrier, inc=1, device_id=(lax.rem(cg + j, n_cg), vg), device_id_type=MESH)
    for j in range(1, n_vg):
        pl.semaphore_signal(barrier, inc=1, device_id=(cg, lax.rem(vg + j, n_vg)), device_id_type=MESH)
    pl.semaphore_wait(barrier, n_cg + n_vg - 2)

    def x_copy(zd):
        return rcopy(to_x.at[zd], from_x.at[zd], x_send.at[zd], x_recv.at[zd], (z * 2 + 1 - x, vg))

    def z_copy(zd, way):
        step = 1 if way == 0 else -1
        return rcopy(
            to_z.at[zd], from_z.at[way, zd], z_send.at[way, zd], z_recv.at[way, zd], ((z + step) * 2 + x, vg)
        )

    def z_arrives(way):
        return z >= 1 if way == 0 else z + 1 < n_z

    order = [(d, way) for d in range(n_z - 1, 0, -1) for way in (0, 1)]

    def place(d, way):
        zd = z + d if way == 0 else z - d
        return zd, (zd >= 0) & (zd < n_z)

    def send_x(zd):
        to_x[zd] = part_ref[rows(zd * 2 + 1 - x, size), :].astype(BF16)
        x_copy(zd).start()

    for d, way in order:
        zd, there = place(d, way)
        pl.when(there)(lambda zd=zd: send_x(zd))
    send_x(z)
    small = Total(n_cg, n_vg, self_ref, grad_self_ref, cuts_a, quarters_a, sem_a)
    small.start()
    column(coef_ref, coef)
    small.second()

    for d, way in order:
        zd, there = place(d, way)

        @pl.when(there)
        def _(zd=zd, way=way):
            x_copy(zd).wait_recv()
            here = part_ref[rows(zd * 2 + x, size), :] + from_x[zd].astype(F32)

            @pl.when(z_arrives(way))
            def _():
                z_copy(zd, way).wait_recv()
                to_z[zd] = (here + from_z[way, zd].astype(F32)).astype(BF16)

            @pl.when(jnp.logical_not(z_arrives(way)))
            def _():
                to_z[zd] = here.astype(BF16)

            z_copy(zd, way).start()

    small.third()
    x_copy(z).wait_recv()
    coef_now = coef[...]
    grad_var_ref[...] = part_ref[rows(cg, size), :] + from_x[z].astype(F32)
    for way in (0, 1):
        @pl.when(z_arrives(way))
        def _(way=way):
            z_copy(z, way).wait_recv()
            grad_var_ref[...] += from_z[way, z].astype(F32)

    coef[...] = grad_var_ref[...] * coef_now
    local_msg[...] = dot(var_ref[...], coef[...], ((0,), (0,)))
    big = Total(n_cg, n_vg, local_msg, grad_msg_ref, cuts_b, quarters_b, sem_b)
    big.start()
    grad_var_ref[...] = dot(coef[...], weight_ref[...], ((1,), (1,)))
    big.second()
    for d, way in order:
        zd, there = place(d, way)
        pl.when(there)(lambda zd=zd, way=way: z_copy(zd, way).wait_send())
    for zd in range(n_z):
        x_copy(zd).wait_send()
    small.finish()
    big.third()
    big.finish()


def last(part, var_embed, msg_weight, col_coef, local_self, n_cg, n_vg):
    size = var_embed.shape[0]
    n_z = n_cg // 2
    n_max = max(n_cg, n_vg)
    cut = H // n_vg
    vmem = pl.BlockSpec(memory_space=pltpu.VMEM)
    square = jax.ShapeDtypeStruct((H, H), F32)
    return pl.pallas_call(
        functools.partial(last_kernel, n_cg, n_vg),
        name="last",
        out_shape=(jax.ShapeDtypeStruct((size, H), F32), square, square),
        in_specs=[vmem] * 5,
        out_specs=(vmem,) * 3,
        scratch_shapes=[
            pltpu.VMEM((size, H), F32),
            pltpu.VMEM((n_z, size, H), BF16),
            pltpu.VMEM((n_z, size, H), BF16),
            pltpu.VMEM((n_z, size, H), BF16),
            pltpu.VMEM((2, n_z, size, H), BF16),
            pltpu.VMEM((H, H), F32),
            pltpu.VMEM((n_vg - 1, cut, H), F32),
            pltpu.VMEM((n_vg - 1, cut, H), F32),
            pltpu.VMEM((n_cg, cut, H), F32),
            pltpu.VMEM((n_cg, cut, H), F32),
            pltpu.SemaphoreType.DMA((n_z,)),
            pltpu.SemaphoreType.DMA((n_z,)),
            pltpu.SemaphoreType.DMA((2, n_z)),
            pltpu.SemaphoreType.DMA((2, n_z)),
            pltpu.SemaphoreType.DMA((6, n_max)),
            pltpu.SemaphoreType.DMA((6, n_max)),
        ],
        compiler_params=pltpu.CompilerParams(collective_id=2, has_side_effects=True),
    )(part, var_embed, msg_weight, col_coef.reshape(-1, H), local_self)


def body(
    con_embed, var_embed, row_coef, col_coef, self_weight, msg_weight,
    timestep, tile_rows, tile_cols, pattern, cotangent,
):
    n_cg, n_vg = lax.axis_size("cg"), lax.axis_size("vg")
    group_rows = con_embed.shape[0] * n_vg
    group_cols = var_embed.shape[0] * n_cg
    row_index = tile_rows.reshape(-1)
    col_index = tile_cols.reshape(-1)
    patterns = pattern.reshape(-1, TB, TB)
    frequency = jnp.exp(-math.log(10000.0) * jnp.arange(H // 2, dtype=F32) / (H // 2))
    phases = timestep[0].astype(F32) * frequency
    time_embed = jnp.concatenate([jnp.sin(phases), jnp.cos(phases)])

    projected = gather_projected(var_embed, msg_weight, col_coef, n_cg)
    forward_sum = tile_sum(row_index, col_index, patterns, projected, group_rows, False)
    con_update, grad_con, local_self, whole_rows = middle(
        forward_sum, con_embed, cotangent, self_weight, row_coef, time_embed, n_vg
    )
    backward_sum = tile_sum(col_index, row_index, patterns, whole_rows, group_cols, True)
    grad_var, grad_msg, grad_self = last(
        backward_sum, var_embed, msg_weight, col_coef, local_self, n_cg, n_vg
    )
    return (con_update, grad_con, grad_var, grad_msg, grad_self)


def solution(mesh):
    in_specs = (
        P(("cg", "vg"), None),
        P(("vg", "cg"), None),
        P(("cg", "vg")),
        P(("vg", "cg")),
        P(),
        P(),
        P(),
        P("cg", "vg", None),
        P("cg", "vg", None),
        P("cg", "vg", None, None, None),
        P(("cg", "vg"), None),
    )
    out_specs = (P(("cg", "vg"), None), P(("cg", "vg"), None), P(("vg", "cg"), None), P(), P())
    return jax.shard_map(body, mesh=mesh, in_specs=in_specs, out_specs=out_specs, check_vma=False)
```

```python
import functools
import math

import jax
import jax.numpy as jnp
from jax import lax
from jax.experimental import pallas as pl
from jax.experimental.pallas import tpu as pltpu
from jax.sharding import PartitionSpec as P

H = 128
TB = 512
CHUNKS = 4
MESH = pl.DeviceIdType.MESH
HIGHEST = lax.Precision.HIGHEST
F32 = jnp.float32
BF16 = jnp.bfloat16


def rcopy(src, dst, send_sem, recv_sem, device):
    return pltpu.make_async_remote_copy(
        src_ref=src, dst_ref=dst, send_sem=send_sem, recv_sem=recv_sem,
        device_id=device, device_id_type=MESH,
    )


def rows(index, size):
    return pl.ds(pl.multiple_of(index * size, size), size)


def dot(a, b, dims=((1,), (0,))):
    return lax.dot_general(a, b, (dims, ((), ())), precision=HIGHEST, preferred_element_type=F32)


def column(coef_ref, out_ref):
    for i in range(coef_ref.shape[0]):
        out_ref[pl.ds(i * H, H), :] = jnp.broadcast_to(coef_ref[pl.ds(i, 1), :], (H, H)).T


class Total:
    def __init__(self, n_cg, n_vg, local, out, cuts, quarters, sem):
        self.n_cg, self.n_vg = n_cg, n_vg
        self.local, self.out, self.cuts, self.quarters, self.sem = local, out, cuts, quarters, sem
        self.cg, self.vg = lax.axis_index("cg"), lax.axis_index("vg")
        self.size = H // n_vg

    def a(self, j):
        v = lax.rem(self.vg + j, self.n_vg)
        return rcopy(
            self.local.at[rows(v, self.size), :], self.cuts.at[j - 1],
            self.sem.at[0, j], self.sem.at[1, j], (self.cg, v),
        )

    def b(self, j):
        c = lax.rem(self.cg + j, self.n_cg)
        block = self.quarters.at[self.cg]
        return rcopy(block, block, self.sem.at[2, j], self.sem.at[3, j], (c, self.vg))

    def b_wait(self, j):
        c = lax.rem(self.cg + self.n_cg - j, self.n_cg)
        block = self.quarters.at[c]
        rcopy(block, block, self.sem.at[2, j], self.sem.at[3, j], (c, self.vg)).wait_recv()

    def c(self, j):
        v = lax.rem(self.vg + j, self.n_vg)
        block = self.out.at[rows(self.vg, self.size), :]
        return rcopy(block, block, self.sem.at[4, j], self.sem.at[5, j], (self.cg, v))

    def c_wait(self, j):
        v = lax.rem(self.vg + self.n_vg - j, self.n_vg)
        block = self.out.at[rows(v, self.size), :]
        rcopy(block, block, self.sem.at[4, j], self.sem.at[5, j], (self.cg, v)).wait_recv()

    def start(self):
        for j in range(1, self.n_vg):
            self.a(j).start()

    def second(self):
        value = self.local[rows(self.vg, self.size), :]
        for j in range(1, self.n_vg):
            self.a(j).wait_recv()
            value = value + self.cuts[j - 1]
        self.quarters[self.cg] = value
        for j in range(1, self.n_cg):
            self.b(j).start()

    def third(self):
        for j in range(1, self.n_cg):
            self.b_wait(j)
            self.b(j).wait_send()
        value = self.quarters[0]
        for c in range(1, self.n_cg):
            value = value + self.quarters[c]
        self.out[rows(self.vg, self.size), :] = value
        for j in range(1, self.n_vg):
            self.c(j).start()

    def finish(self):
        for j in range(1, self.n_vg):
            self.c_wait(j)
            self.c(j).wait_send()
            self.a(j).wait_send()


def layer_kernel(
    n_cg, n_vg, row_ref, col_ref, chain_ref, pattern_hbm, var_ref, msg_w_ref, col_coef_ref, con_hbm, cot_hbm,
    self_w_ref, row_coef_ref, time_ref,
    update_ref, grad_con_ref, grad_var_ref, grad_msg_ref, grad_self_ref,
    pattern, con_ref, cot_ref, coef, pre, projected, whole, acc,
    to_core, from_core, to_peer, from_peer, to_x, from_x, to_z, from_z, local_msg, local_self,
    cuts_a, cuts_b, quarters_a, quarters_b,
    load_sem, gz_send, gx_send, gz_recv, gx_recv,
    core_send, core_recv, peer_send, peer_recv, own_send, pass_send, block_recv, pair_recv,
    x_send, x_recv, z_send, z_recv, sem_a, sem_b,
):
    n_z, n_hi = n_cg // 2, n_vg // 2
    cg, vg = lax.axis_index("cg"), lax.axis_index("vg")
    z, x = cg // 2, cg % 2
    hi, core = vg // 2, vg % 2
    count = pattern.shape[0]
    size = var_ref.shape[0]
    piece = size // CHUNKS
    chunks = range(CHUNKS)
    x_peer, pair = (z * 2 + 1 - x, vg), (cg, hi * 2 + 1 - core)

    barrier = pltpu.get_barrier_semaphore()
    for j in range(1, n_cg):
        pl.semaphore_signal(barrier, inc=1, device_id=(lax.rem(cg + j, n_cg), vg), device_id_type=MESH)
    for j in range(1, n_vg):
        pl.semaphore_signal(barrier, inc=1, device_id=(cg, lax.rem(vg + j, n_vg)), device_id_type=MESH)
    loads = [
        pltpu.make_async_copy(con_hbm, con_ref, load_sem.at[0]),
        pltpu.make_async_copy(cot_hbm, cot_ref, load_sem.at[1]),
        pltpu.make_async_copy(pattern_hbm, pattern, load_sem.at[2]),
    ]
    for load in loads:
        load.start()

    def cut(block, k):
        return rows(block * CHUNKS + k, piece)

    def here(k):
        return pl.ds(k * piece, piece)

    def spot(block, k):
        return block * (size // TB) + (k * piece) // TB, pl.ds((k * piece) % TB, piece)

    def gz_copy(zs, way, k):
        block = projected.at[spot(zs * 2 + x, k)]
        step = 1 if way == 0 else -1
        return rcopy(block, block, gz_send.at[way, zs, k], gz_recv.at[zs, k], ((z + step) * 2 + x, vg))

    def gx_copy(zs, k):
        block = projected.at[spot(zs * 2 + x, k)]
        return rcopy(block, block, gx_send.at[zs, k], gx_recv.at[zs, k], x_peer)

    def gx_wait(zs, k):
        block = projected.at[spot(zs * 2 + 1 - x, k)]
        rcopy(block, block, gx_send.at[zs, k], gx_recv.at[zs, k], x_peer).wait_recv()

    def on(zs, way, act):
        if way == 0:
            pl.when((zs >= 0) & (zs <= z) & (z + 1 < n_z))(act)
        else:
            pl.when((zs < n_z) & (zs >= z) & (z >= 1))(act)

    column(col_coef_ref, coef)
    for k in chunks:
        projected[spot(cg, k)] = (dot(var_ref[here(k), :], msg_w_ref[...]) * coef[here(k), :]).astype(BF16)
        if k == 0:
            pl.semaphore_wait(barrier, n_cg + n_vg - 2)
        for way in (0, 1):
            on(z, way, lambda way=way: gz_copy(z, way, k).start())
        gx_copy(z, k).start()

    acc[count] = jnp.zeros(acc.shape[1:], F32)

    for d in range(1, n_z):
        for k in chunks:
            for way in (0, 1):
                zs = z - d if way == 0 else z + d

                @pl.when((zs >= 0) & (zs < n_z))
                def _(zs=zs, way=way, k=k):
                    gz_copy(zs, way, k).wait_recv()
                    on(zs, way, lambda: gz_copy(zs, way, k).start())
                    gx_copy(zs, k).start()

    for load in loads[:2]:
        load.wait()
    pre[...] = dot(con_ref[...], self_w_ref[...]) + time_ref[...]
    loads[2].wait()
    for k in chunks:
        for zs in range(n_z):
            gx_wait(zs, k)

    row_blocks = whole.shape[0]
    last_f, prev_b, last_b = count, count + row_blocks, 2 * count + row_blocks

    def tile_step(prev, from_ref, source_ref, dims):
        def step(k, carry):
            source = source_ref[from_ref[k]]
            product = lax.dot_general(pattern[k], source, (dims, ((), ())), preferred_element_type=F32)
            acc[k] = product + acc[chain_ref[prev + k]]
            return carry

        lax.fori_loop(0, count, step, 0, unroll=2)

    def part(last, block, k):
        tile = chain_ref[last + block * (size // TB) + (k * piece) // TB]
        return acc[tile, pl.ds((k * piece) % TB, piece), :]

    tile_step(0, col_ref, projected, ((1,), (0,)))

    ups = [lax.rem(hi + j, n_hi) for j in range(n_hi)]
    downs = [lax.rem(hi + n_hi - j, n_hi) for j in range(n_hi)]

    def core_copy(h, k):
        return rcopy(
            to_core.at[cut(h, k), :], from_core.at[cut(h, k), :], core_send.at[h, k], core_recv.at[h, k], pair
        )

    def peer_copy(j, k):
        return rcopy(
            to_peer.at[cut(j - 1, k), :], from_peer.at[cut(j - 1, k), :],
            peer_send.at[j - 1, k], peer_recv.at[j - 1, k], (cg, ups[j] * 2 + core),
        )

    def own_copy(j, k):
        block = whole.at[spot(vg, k)]
        return rcopy(block, block, own_send.at[j - 1, k], block_recv.at[j - 1, k], (cg, ups[j] * 2 + core))

    def block_wait(j, k):
        block = whole.at[spot(downs[j] * 2 + core, k)]
        rcopy(block, block, own_send.at[j - 1, k], block_recv.at[j - 1, k], pair).wait_recv()

    def pass_copy(h, k):
        block = whole.at[spot(h * 2 + core, k)]
        return rcopy(block, block, pass_send.at[h, k], pair_recv.at[h, k], pair)

    def pass_wait(h, k):
        block = whole.at[spot(h * 2 + 1 - core, k)]
        rcopy(block, block, pass_send.at[h, k], pair_recv.at[h, k], pair).wait_recv()

    for j in list(range(1, n_hi)) + [0]:
        for k in chunks:
            to_core[cut(ups[j], k), :] = part(last_f, ups[j] * 2 + 1 - core, k)
            core_copy(ups[j], k).start()
    for j in range(1, n_hi):
        for k in chunks:
            core_copy(ups[j], k).wait_recv()
            to_peer[cut(j - 1, k), :] = (
                part(last_f, ups[j] * 2 + core, k) + from_core[cut(ups[j], k), :]
            ).astype(BF16)
            peer_copy(j, k).start()
    column(row_coef_ref, coef)
    for k in chunks:
        core_copy(hi, k).wait_recv()
        messages = part(last_f, vg, k) + from_core[cut(hi, k), :]
        for j in range(1, n_hi):
            peer_copy(j, k).wait_recv()
            messages = messages + from_peer[cut(j - 1, k), :].astype(F32)
        preact = pre[here(k), :] + coef[here(k), :] * messages
        sig = jax.nn.sigmoid(preact)
        grad_pre = cot_ref[here(k), :] * sig * (1.0 + preact * (1.0 - sig))
        whole[spot(vg, k)] = (coef[here(k), :] * grad_pre).astype(BF16)
        for j in range(1, n_hi):
            own_copy(j, k).start()
        pass_copy(hi, k).start()
        update_ref[here(k), :] = con_ref[here(k), :] + preact * sig
        pre[here(k), :] = grad_pre
    local_self[...] = dot(con_ref[...], pre[...], ((0,), (0,)))
    small = Total(n_cg, n_vg, local_self, grad_self_ref, cuts_a, quarters_a, sem_a)
    small.start()
    grad_con_ref[...] = cot_ref[...] + dot(pre[...], self_w_ref[...], ((1,), (1,)))
    column(col_coef_ref, coef)
    for k in chunks:
        for j in range(1, n_hi):
            block_wait(j, k)
            pass_copy(downs[j], k).start()
    for h in range(n_hi):
        for k in chunks:
            pass_wait(h, k)

    tile_step(prev_b, row_ref, whole, ((0,), (0,)))

    def x_copy(zd, k):
        return rcopy(to_x.at[cut(zd, k), :], from_x.at[cut(zd, k), :], x_send.at[zd, k], x_recv.at[zd, k], x_peer)

    def z_copy(zd, way, k):
        step = 1 if way == 0 else -1
        return rcopy(
            to_z.at[cut(zd, k), :], from_z.at[way, cut(zd, k), :],
            z_send.at[way, zd, k], z_recv.at[way, zd, k], ((z + step) * 2 + x, vg),
        )

    def z_arrives(way):
        return z >= 1 if way == 0 else z + 1 < n_z

    order = [(d, way) for d in range(n_z - 1, 0, -1) for way in (0, 1)]

    def place(d, way):
        zd = z + d if way == 0 else z - d
        return zd, (zd >= 0) & (zd < n_z)

    def send_x(zd):
        for k in chunks:
            to_x[cut(zd, k), :] = part(last_b, zd * 2 + 1 - x, k).astype(BF16)
            x_copy(zd, k).start()

    for d, way in order:
        zd, there = place(d, way)
        pl.when(there)(lambda zd=zd: send_x(zd))
    send_x(z)
    small.second()

    for d, way in order:
        zd, there = place(d, way)

        @pl.when(there)
        def _(zd=zd, way=way):
            for k in chunks:
                x_copy(zd, k).wait_recv()
                value = part(last_b, zd * 2 + x, k) + from_x[cut(zd, k), :].astype(F32)

                @pl.when(z_arrives(way))
                def _(k=k, value=value):
                    z_copy(zd, way, k).wait_recv()
                    to_z[cut(zd, k), :] = (value + from_z[way, cut(zd, k), :].astype(F32)).astype(BF16)

                @pl.when(jnp.logical_not(z_arrives(way)))
                def _(k=k, value=value):
                    to_z[cut(zd, k), :] = value.astype(BF16)

                z_copy(zd, way, k).start()

    small.third()
    for k in chunks:
        x_copy(z, k).wait_recv()
        pre[here(k), :] = part(last_b, cg, k) + from_x[cut(z, k), :].astype(F32)
        for way in (0, 1):
            @pl.when(z_arrives(way))
            def _(way=way, k=k):
                z_copy(z, way, k).wait_recv()
                pre[here(k), :] += from_z[way, cut(z, k), :].astype(F32)

        lin = pre[here(k), :] * coef[here(k), :]
        pre[here(k), :] = lin
        term = dot(var_ref[here(k), :], lin, ((0,), (0,)))
        local_msg[...] = term if k == 0 else local_msg[...] + term
    big = Total(n_cg, n_vg, local_msg, grad_msg_ref, cuts_b, quarters_b, sem_b)
    big.start()
    grad_var_ref[...] = dot(pre[...], msg_w_ref[...], ((1,), (1,)))
    big.second()

    for k in chunks:
        for zs in range(n_z):
            gx_copy(zs, k).wait_send()
            x_copy(zs, k).wait_send()
        for d in range(n_z):
            for way in (0, 1):
                zs = z - d if way == 0 else z + d
                on(zs, way, lambda zs=zs, way=way, k=k: gz_copy(zs, way, k).wait_send())
        for d, way in order:
            zd, there = place(d, way)
            pl.when(there)(lambda zd=zd, way=way, k=k: z_copy(zd, way, k).wait_send())
        for h in range(n_hi):
            pass_copy(h, k).wait_send()
            core_copy(h, k).wait_send()
        for j in range(1, n_hi):
            peer_copy(j, k).wait_send()
            own_copy(j, k).wait_send()
    small.finish()
    big.third()
    big.finish()


def chains_kernel(row_blocks, row_ref, col_ref, out_ref):
    count = row_ref.shape[0]
    base = 0
    for index_ref, blocks in ((row_ref, row_blocks), (col_ref, out_ref.shape[0] - 2 * count - row_blocks)):
        last = base + count

        def clear(b, carry):
            out_ref[last + b] = count
            return carry

        lax.fori_loop(0, blocks, clear, 0)
        for k in range(count):
            at = last + index_ref[k]
            out_ref[base + k] = out_ref[at]
            out_ref[at] = k
        base = last + blocks


def chains(row_index, col_index, row_blocks, col_blocks):
    smem = pl.BlockSpec(memory_space=pltpu.SMEM)
    return pl.pallas_call(
        functools.partial(chains_kernel, row_blocks),
        name="chains",
        out_shape=jax.ShapeDtypeStruct((2 * row_index.shape[0] + row_blocks + col_blocks,), jnp.int32),
        in_specs=[smem] * 2,
        out_specs=smem,
    )(row_index, col_index)


def layer(row_index, col_index, patterns, var_embed, msg_weight, col_coef, con_embed, cotangent,
          self_weight, row_coef, time_embed, n_cg, n_vg):
    size = var_embed.shape[0]
    count = patterns.shape[0]
    n_z, n_hi, n_max = n_cg // 2, n_vg // 2, max(n_cg, n_vg)
    others = max(n_hi - 1, 1)
    row_blocks, col_blocks = n_vg * size // TB, n_cg * size // TB
    share = H // n_vg
    vmem, smem, anywhere = (pl.BlockSpec(memory_space=m) for m in (pltpu.VMEM, pltpu.SMEM, pl.ANY))
    full, square = jax.ShapeDtypeStruct((size, H), F32), jax.ShapeDtypeStruct((H, H), F32)
    dma = lambda *n: pltpu.SemaphoreType.DMA(n)
    return pl.pallas_call(
        functools.partial(layer_kernel, n_cg, n_vg),
        name="layer",
        out_shape=(full, full, full, square, square),
        in_specs=[smem, smem, smem, anywhere, vmem, vmem, vmem, anywhere, anywhere, vmem, vmem, vmem],
        out_specs=(vmem,) * 5,
        scratch_shapes=[
            pltpu.VMEM(patterns.shape, BF16),
            pltpu.VMEM((size, H), F32),
            pltpu.VMEM((size, H), F32),
            pltpu.VMEM((size, H), F32),
            pltpu.VMEM((size, H), F32),
            pltpu.VMEM((col_blocks, TB, H), BF16),
            pltpu.VMEM((row_blocks, TB, H), BF16),
            pltpu.VMEM((count + 1, TB, H), F32),
            pltpu.VMEM((n_hi * size, H), F32),
            pltpu.VMEM((n_hi * size, H), F32),
            pltpu.VMEM((others * size, H), BF16),
            pltpu.VMEM((others * size, H), BF16),
            pltpu.VMEM((n_z * size, H), BF16),
            pltpu.VMEM((n_z * size, H), BF16),
            pltpu.VMEM((n_z * size, H), BF16),
            pltpu.VMEM((2, n_z * size, H), BF16),
            pltpu.VMEM((H, H), F32),
            pltpu.VMEM((H, H), F32),
            pltpu.VMEM((n_vg - 1, share, H), F32),
            pltpu.VMEM((n_vg - 1, share, H), F32),
            pltpu.VMEM((n_cg, share, H), F32),
            pltpu.VMEM((n_cg, share, H), F32),
            dma(3), dma(2, n_z, CHUNKS), dma(n_z, CHUNKS), dma(n_z, CHUNKS), dma(n_z, CHUNKS),
            dma(n_hi, CHUNKS), dma(n_hi, CHUNKS), dma(others, CHUNKS), dma(others, CHUNKS),
            dma(others, CHUNKS), dma(n_hi, CHUNKS), dma(others, CHUNKS), dma(n_hi, CHUNKS),
            dma(n_z, CHUNKS), dma(n_z, CHUNKS), dma(2, n_z, CHUNKS), dma(2, n_z, CHUNKS),
            dma(6, n_max), dma(6, n_max),
        ],
        compiler_params=pltpu.CompilerParams(
            collective_id=0, has_side_effects=True, vmem_limit_bytes=60000 * 1024
        ),
    )(
        row_index, col_index, chains(row_index, col_index, row_blocks, col_blocks), patterns, var_embed, msg_weight, col_coef.reshape(-1, H),
        con_embed, cotangent, self_weight, row_coef.reshape(-1, H), time_embed.reshape(1, H),
    )


def finish_kernel(*refs):
    half = len(refs) // 2
    for source, target in zip(refs[:half], refs[half:]):
        target[...] = source[...]


def finish(*arrays):
    steps = 2
    specs = [pl.BlockSpec((a.shape[0] // steps, H), lambda i: (i, 0)) for a in arrays]
    return pl.pallas_call(
        finish_kernel,
        name="finish",
        grid=(steps,),
        out_shape=tuple(jax.ShapeDtypeStruct(a.shape, a.dtype) for a in arrays),
        in_specs=specs,
        out_specs=tuple(specs),
    )(*arrays)


def body(
    con_embed, var_embed, row_coef, col_coef, self_weight, msg_weight,
    timestep, tile_rows, tile_cols, pattern, cotangent,
):
    n_cg, n_vg = lax.axis_size("cg"), lax.axis_size("vg")
    frequency = jnp.exp(-math.log(10000.0) * jnp.arange(H // 2, dtype=F32) / (H // 2))
    phases = timestep[0].astype(F32) * frequency
    time_embed = jnp.concatenate([jnp.sin(phases), jnp.cos(phases)])
    return finish(*layer(
        tile_rows.reshape(-1), tile_cols.reshape(-1), pattern.reshape(-1, TB, TB), var_embed, msg_weight,
        col_coef, con_embed, cotangent, self_weight, row_coef, time_embed, n_cg, n_vg,
    ))


def solution(mesh):
    in_specs = (
        P(("cg", "vg"), None),
        P(("vg", "cg"), None),
        P(("cg", "vg")),
        P(("vg", "cg")),
        P(),
        P(),
        P(),
        P("cg", "vg", None),
        P("cg", "vg", None),
        P("cg", "vg", None, None, None),
        P(("cg", "vg"), None),
    )
    out_specs = (P(("cg", "vg"), None), P(("cg", "vg"), None), P(("vg", "cg"), None), P(), P())
    return jax.shard_map(body, mesh=mesh, in_specs=in_specs, out_specs=out_specs, check_vma=False)
```

```python
import functools
import math

import jax
import jax.numpy as jnp
from jax import lax
from jax.experimental import pallas as pl
from jax.experimental.pallas import tpu as pltpu
from jax.sharding import PartitionSpec as P

H = 128
TB = 512
CHUNKS = 4
EARLY = 1
MESH = pl.DeviceIdType.MESH
HIGHEST = lax.Precision.HIGHEST
F32 = jnp.float32
BF16 = jnp.bfloat16


def rcopy(src, dst, send_sem, recv_sem, device):
    return pltpu.make_async_remote_copy(
        src_ref=src, dst_ref=dst, send_sem=send_sem, recv_sem=recv_sem,
        device_id=device, device_id_type=MESH,
    )


def rows(index, size):
    return pl.ds(pl.multiple_of(index * size, size), size)


def dot(a, b, dims=((1,), (0,))):
    return lax.dot_general(a, b, (dims, ((), ())), precision=HIGHEST, preferred_element_type=F32)


def column(coef_ref, out_ref):
    for i in range(coef_ref.shape[0]):
        out_ref[pl.ds(i * H, H), :] = jnp.broadcast_to(coef_ref[pl.ds(i, 1), :], (H, H)).T


class Total:
    def __init__(self, n_cg, n_vg, local, out, cuts, quarters, sem):
        self.n_cg, self.n_vg = n_cg, n_vg
        self.local, self.out, self.cuts, self.quarters, self.sem = local, out, cuts, quarters, sem
        self.cg, self.vg = lax.axis_index("cg"), lax.axis_index("vg")
        self.size = H // n_vg

    def a(self, j):
        v = lax.rem(self.vg + j, self.n_vg)
        return rcopy(
            self.local.at[rows(v, self.size), :], self.cuts.at[j - 1],
            self.sem.at[0, j], self.sem.at[1, j], (self.cg, v),
        )

    def b(self, j):
        c = lax.rem(self.cg + j, self.n_cg)
        block = self.quarters.at[self.cg]
        return rcopy(block, block, self.sem.at[2, j], self.sem.at[3, j], (c, self.vg))

    def b_wait(self, j):
        c = lax.rem(self.cg + self.n_cg - j, self.n_cg)
        block = self.quarters.at[c]
        rcopy(block, block, self.sem.at[2, j], self.sem.at[3, j], (c, self.vg)).wait_recv()

    def c(self, j):
        v = lax.rem(self.vg + j, self.n_vg)
        block = self.out.at[rows(self.vg, self.size), :]
        return rcopy(block, block, self.sem.at[4, j], self.sem.at[5, j], (self.cg, v))

    def c_wait(self, j):
        v = lax.rem(self.vg + self.n_vg - j, self.n_vg)
        block = self.out.at[rows(v, self.size), :]
        rcopy(block, block, self.sem.at[4, j], self.sem.at[5, j], (self.cg, v)).wait_recv()

    def start(self):
        for j in range(1, self.n_vg):
            self.a(j).start()

    def second(self):
        value = self.local[rows(self.vg, self.size), :]
        for j in range(1, self.n_vg):
            self.a(j).wait_recv()
            value = value + self.cuts[j - 1]
        self.quarters[self.cg] = value
        for j in range(1, self.n_cg):
            self.b(j).start()

    def third(self):
        for j in range(1, self.n_cg):
            self.b_wait(j)
            self.b(j).wait_send()
        value = self.quarters[0]
        for c in range(1, self.n_cg):
            value = value + self.quarters[c]
        self.out[rows(self.vg, self.size), :] = value
        for j in range(1, self.n_vg):
            self.c(j).start()

    def finish(self):
        for j in range(1, self.n_vg):
            self.c_wait(j)
            self.c(j).wait_send()
            self.a(j).wait_send()


def layer_kernel(
    n_cg, n_vg, row_ref, col_ref, chain_ref, pattern_hbm, var_ref, msg_w_ref, col_coef_ref, con_hbm, cot_hbm,
    self_w_ref, row_coef_ref, time_ref,
    update_ref, grad_con_ref, grad_var_ref, grad_msg_ref, grad_self_ref,
    pattern, con_ref, cot_ref, coef, pre, projected, whole, acc,
    to_core, from_core, to_peer, from_peer, to_x, from_x, to_z, from_z, local_msg, local_self,
    cuts_a, cuts_b, quarters_a, quarters_b,
    load_sem, gz_send, gx_send, gz_recv, gx_recv,
    core_send, core_recv, peer_send, peer_recv, own_send, pass_send, block_recv, pair_recv,
    x_send, x_recv, z_send, z_recv, sem_a, sem_b,
):
    n_z, n_hi = n_cg // 2, n_vg // 2
    cg, vg = lax.axis_index("cg"), lax.axis_index("vg")
    z, x = cg // 2, cg % 2
    hi, core = vg // 2, vg % 2
    count = pattern.shape[0]
    size = var_ref.shape[0]
    piece = size // CHUNKS
    chunks = range(CHUNKS)
    x_peer, pair = (z * 2 + 1 - x, vg), (cg, hi * 2 + 1 - core)

    barrier = pltpu.get_barrier_semaphore()
    for j in range(1, n_cg):
        pl.semaphore_signal(barrier, inc=1, device_id=(lax.rem(cg + j, n_cg), vg), device_id_type=MESH)
    for j in range(1, n_vg):
        pl.semaphore_signal(barrier, inc=1, device_id=(cg, lax.rem(vg + j, n_vg)), device_id_type=MESH)
    loads = [
        pltpu.make_async_copy(con_hbm, con_ref, load_sem.at[0]),
        pltpu.make_async_copy(cot_hbm, cot_ref, load_sem.at[1]),
        pltpu.make_async_copy(pattern_hbm, pattern, load_sem.at[2]),
    ]
    for load in loads:
        load.start()

    def cut(block, k):
        return rows(block * CHUNKS + k, piece)

    def here(k):
        return pl.ds(k * piece, piece)

    def spot(block, k):
        return block * (size // TB) + (k * piece) // TB, pl.ds((k * piece) % TB, piece)

    def gz_copy(zs, way, k, other=0):
        block = projected.at[spot(zs * 2 + (1 - x if other else x), k)]
        step = 1 if way == 0 else -1
        slot = k + other * CHUNKS
        return rcopy(block, block, gz_send.at[way, zs, slot], gz_recv.at[zs, slot], ((z + step) * 2 + x, vg))

    def gx_copy(zs, k):
        block = projected.at[spot(zs * 2 + x, k)]
        return rcopy(block, block, gx_send.at[zs, k], gx_recv.at[zs, k], x_peer)

    def gx_wait(zs, k):
        block = projected.at[spot(zs * 2 + 1 - x, k)]
        rcopy(block, block, gx_send.at[zs, k], gx_recv.at[zs, k], x_peer).wait_recv()

    def on(zs, way, act):
        if way == 0:
            pl.when((zs >= 0) & (zs <= z) & (z + 1 < n_z))(act)
        else:
            pl.when((zs < n_z) & (zs >= z) & (z >= 1))(act)

    column(col_coef_ref, coef)
    for k in chunks:
        projected[spot(cg, k)] = (dot(var_ref[here(k), :], msg_w_ref[...]) * coef[here(k), :]).astype(BF16)
        if k == 0:
            pl.semaphore_wait(barrier, n_cg + n_vg - 2)
        for way in (0, 1):
            on(z, way, lambda way=way: gz_copy(z, way, k).start())
        gx_copy(z, k).start()
    for k in range(EARLY):
        gx_wait(z, k)
        for way in (0, 1):
            on(z, way, lambda way=way, k=k: gz_copy(z, way, k, 1).start())

    acc[count] = jnp.zeros(acc.shape[1:], F32)

    for d in range(1, n_z):
        for k in chunks:
            for way in (0, 1):
                zs = z - d if way == 0 else z + d

                @pl.when((zs >= 0) & (zs < n_z))
                def _(zs=zs, way=way, k=k):
                    gz_copy(zs, way, k).wait_recv()
                    on(zs, way, lambda: gz_copy(zs, way, k).start())
                    if k < EARLY:
                        gz_copy(zs, way, k, 1).wait_recv()
                        on(zs, way, lambda: gz_copy(zs, way, k, 1).start())
                    else:
                        gx_copy(zs, k).start()

    for load in loads[:2]:
        load.wait()
    pre[...] = dot(con_ref[...], self_w_ref[...]) + time_ref[...]
    loads[2].wait()
    for k in range(EARLY, CHUNKS):
        for zs in range(n_z):
            gx_wait(zs, k)

    row_blocks = whole.shape[0]
    last_f, prev_b, last_b = count, count + row_blocks, 2 * count + row_blocks

    def tile_step(prev, from_ref, source_ref, dims):
        def step(k, carry):
            source = source_ref[from_ref[k]]
            product = lax.dot_general(pattern[k], source, (dims, ((), ())), preferred_element_type=F32)
            acc[k] = product + acc[chain_ref[prev + k]]
            return carry

        lax.fori_loop(0, count, step, 0, unroll=4)

    def part(last, block, k):
        tile = chain_ref[last + block * (size // TB) + (k * piece) // TB]
        return acc[tile, pl.ds((k * piece) % TB, piece), :]

    tile_step(0, col_ref, projected, ((1,), (0,)))

    ups = [lax.rem(hi + j, n_hi) for j in range(n_hi)]
    downs = [lax.rem(hi + n_hi - j, n_hi) for j in range(n_hi)]

    def core_copy(h, k):
        return rcopy(
            to_core.at[cut(h, k), :], from_core.at[cut(h, k), :], core_send.at[h, k], core_recv.at[h, k], pair
        )

    def peer_copy(j, k):
        return rcopy(
            to_peer.at[cut(j - 1, k), :], from_peer.at[cut(j - 1, k), :],
            peer_send.at[j - 1, k], peer_recv.at[j - 1, k], (cg, ups[j] * 2 + core),
        )

    def own_copy(j, k):
        block = whole.at[spot(vg, k)]
        return rcopy(block, block, own_send.at[j - 1, k], block_recv.at[j - 1, k], (cg, ups[j] * 2 + core))

    def block_wait(j, k):
        block = whole.at[spot(downs[j] * 2 + core, k)]
        rcopy(block, block, own_send.at[j - 1, k], block_recv.at[j - 1, k], pair).wait_recv()

    def pass_copy(h, k):
        block = whole.at[spot(h * 2 + core, k)]
        return rcopy(block, block, pass_send.at[h, k], pair_recv.at[h, k], pair)

    def pass_wait(h, k):
        block = whole.at[spot(h * 2 + 1 - core, k)]
        rcopy(block, block, pass_send.at[h, k], pair_recv.at[h, k], pair).wait_recv()

    for j in list(range(1, n_hi)) + [0]:
        for k in chunks:
            to_core[cut(ups[j], k), :] = part(last_f, ups[j] * 2 + 1 - core, k)
            core_copy(ups[j], k).start()
    for j in range(1, n_hi):
        for k in chunks:
            core_copy(ups[j], k).wait_recv()
            to_peer[cut(j - 1, k), :] = (
                part(last_f, ups[j] * 2 + core, k) + from_core[cut(ups[j], k), :]
            ).astype(BF16)
            peer_copy(j, k).start()
    column(row_coef_ref, coef)
    for k in chunks:
        core_copy(hi, k).wait_recv()
        messages = part(last_f, vg, k) + from_core[cut(hi, k), :]
        for j in range(1, n_hi):
            peer_copy(j, k).wait_recv()
            messages = messages + from_peer[cut(j - 1, k), :].astype(F32)
        preact = pre[here(k), :] + coef[here(k), :] * messages
        sig = jax.nn.sigmoid(preact)
        grad_pre = cot_ref[here(k), :] * sig * (1.0 + preact * (1.0 - sig))
        whole[spot(vg, k)] = (coef[here(k), :] * grad_pre).astype(BF16)
        for j in range(1, n_hi):
            own_copy(j, k).start()
        pass_copy(hi, k).start()
        update_ref[here(k), :] = con_ref[here(k), :] + preact * sig
        pre[here(k), :] = grad_pre
    local_self[...] = dot(con_ref[...], pre[...], ((0,), (0,)))
    small = Total(n_cg, n_vg, local_self, grad_self_ref, cuts_a, quarters_a, sem_a)
    small.start()
    grad_con_ref[...] = cot_ref[...] + dot(pre[...], self_w_ref[...], ((1,), (1,)))
    column(col_coef_ref, coef)
    for k in chunks:
        for j in range(1, n_hi):
            block_wait(j, k)
            pass_copy(downs[j], k).start()
    for h in range(n_hi):
        for k in chunks:
            pass_wait(h, k)

    tile_step(prev_b, row_ref, whole, ((0,), (0,)))

    def x_copy(zd, k):
        return rcopy(to_x.at[cut(zd, k), :], from_x.at[cut(zd, k), :], x_send.at[zd, k], x_recv.at[zd, k], x_peer)

    def z_cut(zd, k, other):
        return cut(zd, k) if other == 0 else pl.ds(pl.multiple_of(late + (zd * EARLY + k) * piece, piece), piece)

    late = n_z * size

    def z_copy(zd, way, k, other=0):
        step = 1 if way == 0 else -1
        slot = k + other * CHUNKS
        return rcopy(
            to_z.at[z_cut(zd, k, other), :], from_z.at[way, z_cut(zd, k, other), :],
            z_send.at[way, zd, slot], z_recv.at[way, zd, slot], ((z + step) * 2 + x, vg),
        )

    def z_arrives(way):
        return z >= 1 if way == 0 else z + 1 < n_z

    order = [(d, way) for d in range(n_z - 1, 0, -1) for way in (0, 1)]

    def place(d, way):
        zd = z + d if way == 0 else z - d
        return zd, (zd >= 0) & (zd < n_z)

    def send_x(zd):
        for k in range(EARLY, CHUNKS):
            to_x[cut(zd, k), :] = part(last_b, zd * 2 + 1 - x, k).astype(BF16)
            x_copy(zd, k).start()

    def send_z(zd, way, k, other=0):
        value = part(last_b, zd * 2 + (1 - x if other else x), k)
        if k >= EARLY:
            value = value + from_x[cut(zd, k), :].astype(F32)

        @pl.when(z_arrives(way))
        def _():
            z_copy(zd, way, k, other).wait_recv()
            to_z[z_cut(zd, k, other), :] = (
                value + from_z[way, z_cut(zd, k, other), :].astype(F32)
            ).astype(BF16)

        @pl.when(jnp.logical_not(z_arrives(way)))
        def _():
            to_z[z_cut(zd, k, other), :] = value.astype(BF16)

        z_copy(zd, way, k, other).start()

    def arrived(k, other):
        for way in (0, 1):
            @pl.when(z_arrives(way))
            def _(way=way):
                z_copy(z, way, k, other).wait_recv()
                pre[here(k), :] += from_z[way, z_cut(z, k, other), :].astype(F32)

    for d, way in order:
        zd, there = place(d, way)
        pl.when(there)(lambda zd=zd: send_x(zd))
    send_x(z)
    small.second()

    for d, way in order:
        zd, there = place(d, way)

        @pl.when(there)
        def _(zd=zd, way=way):
            for k in range(EARLY):
                for other in (0, 1):
                    send_z(zd, way, k, other)
            for k in range(EARLY, CHUNKS):
                x_copy(zd, k).wait_recv()
                send_z(zd, way, k)

    small.third()
    for k in range(EARLY):
        pre[here(k), :] = part(last_b, z * 2 + 1 - x, k)
        arrived(k, 1)
        to_x[cut(z, k), :] = pre[here(k), :].astype(BF16)
        x_copy(z, k).start()
    for k in list(range(EARLY, CHUNKS)) + list(range(EARLY)):
        x_copy(z, k).wait_recv()
        pre[here(k), :] = part(last_b, cg, k) + from_x[cut(z, k), :].astype(F32)
        arrived(k, 0)
        lin = pre[here(k), :] * coef[here(k), :]
        pre[here(k), :] = lin
        term = dot(var_ref[here(k), :], lin, ((0,), (0,)))
        local_msg[...] = term if k == EARLY else local_msg[...] + term
    big = Total(n_cg, n_vg, local_msg, grad_msg_ref, cuts_b, quarters_b, sem_b)
    big.start()
    grad_var_ref[...] = dot(pre[...], msg_w_ref[...], ((1,), (1,)))
    big.second()

    for k in chunks:
        if k < EARLY:
            gx_copy(z, k).wait_send()
            x_copy(z, k).wait_send()
        else:
            for zs in range(n_z):
                gx_copy(zs, k).wait_send()
                x_copy(zs, k).wait_send()
        for d in range(n_z):
            for way in (0, 1):
                zs = z - d if way == 0 else z + d
                for other in (0, 1) if k < EARLY else (0,):
                    on(zs, way, lambda zs=zs, way=way, k=k, o=other: gz_copy(zs, way, k, o).wait_send())
        for d, way in order:
            zd, there = place(d, way)
            for other in (0, 1) if k < EARLY else (0,):
                pl.when(there)(lambda zd=zd, way=way, k=k, o=other: z_copy(zd, way, k, o).wait_send())
        for h in range(n_hi):
            pass_copy(h, k).wait_send()
            core_copy(h, k).wait_send()
        for j in range(1, n_hi):
            peer_copy(j, k).wait_send()
            own_copy(j, k).wait_send()
    small.finish()
    big.third()
    big.finish()


def chains_kernel(row_blocks, row_ref, col_ref, out_ref):
    count = row_ref.shape[0]
    base = 0
    for index_ref, blocks in ((row_ref, row_blocks), (col_ref, out_ref.shape[0] - 2 * count - row_blocks)):
        last = base + count

        def clear(b, carry):
            out_ref[last + b] = count
            return carry

        lax.fori_loop(0, blocks, clear, 0)
        for k in range(count):
            at = last + index_ref[k]
            out_ref[base + k] = out_ref[at]
            out_ref[at] = k
        base = last + blocks


def chains(row_index, col_index, row_blocks, col_blocks):
    smem = pl.BlockSpec(memory_space=pltpu.SMEM)
    return pl.pallas_call(
        functools.partial(chains_kernel, row_blocks),
        name="chains",
        out_shape=jax.ShapeDtypeStruct((2 * row_index.shape[0] + row_blocks + col_blocks,), jnp.int32),
        in_specs=[smem] * 2,
        out_specs=smem,
    )(row_index, col_index)


def layer(row_index, col_index, patterns, var_embed, msg_weight, col_coef, con_embed, cotangent,
          self_weight, row_coef, time_embed, n_cg, n_vg):
    size = var_embed.shape[0]
    count = patterns.shape[0]
    n_z, n_hi, n_max = n_cg // 2, n_vg // 2, max(n_cg, n_vg)
    others = max(n_hi - 1, 1)
    row_blocks, col_blocks = n_vg * size // TB, n_cg * size // TB
    share = H // n_vg
    extra = EARLY * (size // CHUNKS)
    slots = CHUNKS + EARLY
    vmem, smem, anywhere = (pl.BlockSpec(memory_space=m) for m in (pltpu.VMEM, pltpu.SMEM, pl.ANY))
    full, square = jax.ShapeDtypeStruct((size, H), F32), jax.ShapeDtypeStruct((H, H), F32)
    dma = lambda *n: pltpu.SemaphoreType.DMA(n)
    return pl.pallas_call(
        functools.partial(layer_kernel, n_cg, n_vg),
        name="layer",
        out_shape=(full, full, full, square, square),
        in_specs=[smem, smem, smem, anywhere, vmem, vmem, vmem, anywhere, anywhere, vmem, vmem, vmem],
        out_specs=(vmem,) * 5,
        scratch_shapes=[
            pltpu.VMEM(patterns.shape, BF16),
            pltpu.VMEM((size, H), F32),
            pltpu.VMEM((size, H), F32),
            pltpu.VMEM((size, H), F32),
            pltpu.VMEM((size, H), F32),
            pltpu.VMEM((col_blocks, TB, H), BF16),
            pltpu.VMEM((row_blocks, TB, H), BF16),
            pltpu.VMEM((count + 1, TB, H), F32),
            pltpu.VMEM((n_hi * size, H), F32),
            pltpu.VMEM((n_hi * size, H), F32),
            pltpu.VMEM((others * size, H), BF16),
            pltpu.VMEM((others * size, H), BF16),
            pltpu.VMEM((n_z * size, H), BF16),
            pltpu.VMEM((n_z * size, H), BF16),
            pltpu.VMEM((n_z * (size + extra), H), BF16),
            pltpu.VMEM((2, n_z * (size + extra), H), BF16),
            pltpu.VMEM((H, H), F32),
            pltpu.VMEM((H, H), F32),
            pltpu.VMEM((n_vg - 1, share, H), F32),
            pltpu.VMEM((n_vg - 1, share, H), F32),
            pltpu.VMEM((n_cg, share, H), F32),
            pltpu.VMEM((n_cg, share, H), F32),
            dma(3), dma(2, n_z, slots), dma(n_z, CHUNKS), dma(n_z, slots), dma(n_z, CHUNKS),
            dma(n_hi, CHUNKS), dma(n_hi, CHUNKS), dma(others, CHUNKS), dma(others, CHUNKS),
            dma(others, CHUNKS), dma(n_hi, CHUNKS), dma(others, CHUNKS), dma(n_hi, CHUNKS),
            dma(n_z, CHUNKS), dma(n_z, CHUNKS), dma(2, n_z, slots), dma(2, n_z, slots),
            dma(6, n_max), dma(6, n_max),
        ],
        compiler_params=pltpu.CompilerParams(
            collective_id=0, has_side_effects=True, vmem_limit_bytes=60000 * 1024
        ),
    )(
        row_index, col_index, chains(row_index, col_index, row_blocks, col_blocks), patterns, var_embed, msg_weight, col_coef.reshape(-1, H),
        con_embed, cotangent, self_weight, row_coef.reshape(-1, H), time_embed.reshape(1, H),
    )


def finish_kernel(*refs):
    half = len(refs) // 2
    for source, target in zip(refs[:half], refs[half:]):
        target[...] = source[...]


def finish(*arrays):
    steps = 2
    specs = [pl.BlockSpec((a.shape[0] // steps, H), lambda i: (i, 0)) for a in arrays]
    return pl.pallas_call(
        finish_kernel,
        name="finish",
        grid=(steps,),
        out_shape=tuple(jax.ShapeDtypeStruct(a.shape, a.dtype) for a in arrays),
        in_specs=specs,
        out_specs=tuple(specs),
    )(*arrays)


def body(
    con_embed, var_embed, row_coef, col_coef, self_weight, msg_weight,
    timestep, tile_rows, tile_cols, pattern, cotangent,
):
    n_cg, n_vg = lax.axis_size("cg"), lax.axis_size("vg")
    frequency = jnp.exp(-math.log(10000.0) * jnp.arange(H // 2, dtype=F32) / (H // 2))
    phases = timestep[0].astype(F32) * frequency
    time_embed = jnp.concatenate([jnp.sin(phases), jnp.cos(phases)])
    return finish(*layer(
        tile_rows.reshape(-1), tile_cols.reshape(-1), pattern.reshape(-1, TB, TB), var_embed, msg_weight,
        col_coef, con_embed, cotangent, self_weight, row_coef, time_embed, n_cg, n_vg,
    ))


def solution(mesh):
    in_specs = (
        P(("cg", "vg"), None),
        P(("vg", "cg"), None),
        P(("cg", "vg")),
        P(("vg", "cg")),
        P(),
        P(),
        P(),
        P("cg", "vg", None),
        P("cg", "vg", None),
        P("cg", "vg", None, None, None),
        P(("cg", "vg"), None),
    )
    out_specs = (P(("cg", "vg"), None), P(("cg", "vg"), None), P(("vg", "cg"), None), P(), P())
    return jax.shard_map(body, mesh=mesh, in_specs=in_specs, out_specs=out_specs, check_vma=False)
```

```python
import functools
import math

import jax
import jax.numpy as jnp
from jax import lax
from jax.experimental import pallas as pl
from jax.experimental.pallas import tpu as pltpu
from jax.sharding import PartitionSpec as P

H = 128
TB = 512
CHUNKS = 4
MESH = pl.DeviceIdType.MESH
HIGHEST = lax.Precision.HIGHEST
F32 = jnp.float32
BF16 = jnp.bfloat16


def rcopy(src, dst, send_sem, recv_sem, device):
    return pltpu.make_async_remote_copy(
        src_ref=src, dst_ref=dst, send_sem=send_sem, recv_sem=recv_sem,
        device_id=device, device_id_type=MESH,
    )


def rows(index, size):
    return pl.ds(pl.multiple_of(index * size, size), size)


def dot(a, b, dims=((1,), (0,))):
    return lax.dot_general(a, b, (dims, ((), ())), precision=HIGHEST, preferred_element_type=F32)


def column(coef_ref, out_ref):
    for i in range(coef_ref.shape[0]):
        out_ref[pl.ds(i * H, H), :] = jnp.broadcast_to(coef_ref[pl.ds(i, 1), :], (H, H)).T


class Total:
    def __init__(self, n_cg, n_vg, local, out, cuts, quarters, sem):
        self.n_cg, self.n_vg = n_cg, n_vg
        self.local, self.out, self.cuts, self.quarters, self.sem = local, out, cuts, quarters, sem
        self.cg, self.vg = lax.axis_index("cg"), lax.axis_index("vg")
        self.size = H // n_vg

    def a(self, j):
        v = lax.rem(self.vg + j, self.n_vg)
        return rcopy(
            self.local.at[rows(v, self.size), :], self.cuts.at[j - 1],
            self.sem.at[0, j], self.sem.at[1, j], (self.cg, v),
        )

    def b(self, j):
        c = lax.rem(self.cg + j, self.n_cg)
        block = self.quarters.at[self.cg]
        return rcopy(block, block, self.sem.at[2, j], self.sem.at[3, j], (c, self.vg))

    def b_wait(self, j):
        c = lax.rem(self.cg + self.n_cg - j, self.n_cg)
        block = self.quarters.at[c]
        rcopy(block, block, self.sem.at[2, j], self.sem.at[3, j], (c, self.vg)).wait_recv()

    def c(self, j):
        v = lax.rem(self.vg + j, self.n_vg)
        block = self.out.at[rows(self.vg, self.size), :]
        return rcopy(block, block, self.sem.at[4, j], self.sem.at[5, j], (self.cg, v))

    def c_wait(self, j):
        v = lax.rem(self.vg + self.n_vg - j, self.n_vg)
        block = self.out.at[rows(v, self.size), :]
        rcopy(block, block, self.sem.at[4, j], self.sem.at[5, j], (self.cg, v)).wait_recv()

    def start(self):
        for j in range(1, self.n_vg):
            self.a(j).start()

    def second(self):
        value = self.local[rows(self.vg, self.size), :]
        for j in range(1, self.n_vg):
            self.a(j).wait_recv()
            value = value + self.cuts[j - 1]
        self.quarters[self.cg] = value
        for j in range(1, self.n_cg):
            self.b(j).start()

    def third(self):
        for j in range(1, self.n_cg):
            self.b_wait(j)
            self.b(j).wait_send()
        value = self.quarters[0]
        for c in range(1, self.n_cg):
            value = value + self.quarters[c]
        self.out[rows(self.vg, self.size), :] = value
        for j in range(1, self.n_vg):
            self.c(j).start()

    def finish(self):
        for j in range(1, self.n_vg):
            self.c_wait(j)
            self.c(j).wait_send()
            self.a(j).wait_send()


def layer_kernel(
    n_cg, n_vg, row_ref, col_ref, chain_ref, pattern_hbm, var_ref, msg_w_ref, col_coef_ref, con_hbm, cot_hbm,
    self_w_ref, row_coef_ref, time_ref,
    update_ref, grad_con_ref, grad_var_ref, grad_msg_ref, grad_self_ref,
    pattern, con_ref, cot_ref, coef, pre, projected, whole, acc,
    to_core, from_core, to_peer, from_peer, to_x, from_x, to_z, from_z, local_msg, local_self,
    cuts_a, cuts_b, quarters_a, quarters_b,
    load_sem, gz_send, gx_send, gz_recv, gx_recv,
    core_send, core_recv, peer_send, peer_recv, own_send, pass_send, block_recv, pair_recv,
    x_send, x_recv, z_send, z_recv, sem_a, sem_b,
):
    n_z, n_hi = n_cg // 2, n_vg // 2
    cg, vg = lax.axis_index("cg"), lax.axis_index("vg")
    z, x = cg // 2, cg % 2
    hi, core = vg // 2, vg % 2
    count = pattern.shape[0]
    size = var_ref.shape[0]
    piece = size // CHUNKS
    chunks = range(CHUNKS)
    x_peer, pair = (z * 2 + 1 - x, vg), (cg, hi * 2 + 1 - core)

    barrier = pltpu.get_barrier_semaphore()
    for j in range(1, n_cg):
        pl.semaphore_signal(barrier, inc=1, device_id=(lax.rem(cg + j, n_cg), vg), device_id_type=MESH)
    for j in range(1, n_vg):
        pl.semaphore_signal(barrier, inc=1, device_id=(cg, lax.rem(vg + j, n_vg)), device_id_type=MESH)
    loads = [
        pltpu.make_async_copy(con_hbm, con_ref, load_sem.at[0]),
        pltpu.make_async_copy(cot_hbm, cot_ref, load_sem.at[1]),
        pltpu.make_async_copy(pattern_hbm, pattern, load_sem.at[2]),
    ]
    for load in loads:
        load.start()

    def cut(block, k):
        return rows(block * CHUNKS + k, piece)

    def here(k):
        return pl.ds(k * piece, piece)

    def spot(block, k):
        return block * (size // TB) + (k * piece) // TB, pl.ds((k * piece) % TB, piece)

    def gz_copy(zs, way, k):
        block = projected.at[spot(zs * 2 + x, k)]
        step = 1 if way == 0 else -1
        return rcopy(block, block, gz_send.at[way, zs, k], gz_recv.at[zs, k], ((z + step) * 2 + x, vg))

    def gx_copy(zs, k):
        block = projected.at[spot(zs * 2 + x, k)]
        return rcopy(block, block, gx_send.at[zs, k], gx_recv.at[zs, k], x_peer)

    def gx_wait(zs, k):
        block = projected.at[spot(zs * 2 + 1 - x, k)]
        rcopy(block, block, gx_send.at[zs, k], gx_recv.at[zs, k], x_peer).wait_recv()

    def on(zs, way, act):
        if way == 0:
            pl.when((zs >= 0) & (zs <= z) & (z + 1 < n_z))(act)
        else:
            pl.when((zs < n_z) & (zs >= z) & (z >= 1))(act)

    column(col_coef_ref, coef)
    for k in chunks:
        projected[spot(cg, k)] = (dot(var_ref[here(k), :], msg_w_ref[...]) * coef[here(k), :]).astype(BF16)
        if k == 0:
            pl.semaphore_wait(barrier, n_cg + n_vg - 2)
        for way in (0, 1):
            on(z, way, lambda way=way: gz_copy(z, way, k).start())
        gx_copy(z, k).start()

    acc[count] = jnp.zeros(acc.shape[1:], F32)

    for d in range(1, n_z):
        for k in chunks:
            for way in (0, 1):
                zs = z - d if way == 0 else z + d

                @pl.when((zs >= 0) & (zs < n_z))
                def _(zs=zs, way=way, k=k):
                    gz_copy(zs, way, k).wait_recv()
                    on(zs, way, lambda: gz_copy(zs, way, k).start())
                    gx_copy(zs, k).start()

    for load in loads[:2]:
        load.wait()
    pre[...] = dot(con_ref[...], self_w_ref[...]) + time_ref[...]
    loads[2].wait()
    for k in chunks:
        for zs in range(n_z):
            gx_wait(zs, k)

    row_blocks = whole.shape[0]
    last_f, prev_b, last_b = count, count + row_blocks, 2 * count + row_blocks

    def tile_step(prev, from_ref, source_ref, dims):
        def step(k, carry):
            source = source_ref[from_ref[k]]
            product = lax.dot_general(pattern[k], source, (dims, ((), ())), preferred_element_type=F32)
            acc[k] = product + acc[chain_ref[prev + k]]
            return carry

        lax.fori_loop(0, count, step, 0, unroll=4)

    def part(last, block, k):
        tile = chain_ref[last + block * (size // TB) + (k * piece) // TB]
        return acc[tile, pl.ds((k * piece) % TB, piece), :]

    tile_step(0, col_ref, projected, ((1,), (0,)))

    ups = [lax.rem(hi + j, n_hi) for j in range(n_hi)]
    downs = [lax.rem(hi + n_hi - j, n_hi) for j in range(n_hi)]

    def core_copy(h, k):
        return rcopy(
            to_core.at[cut(h, k), :], from_core.at[cut(h, k), :], core_send.at[h, k], core_recv.at[h, k], pair
        )

    def peer_copy(j, k):
        return rcopy(
            to_peer.at[cut(j - 1, k), :], from_peer.at[cut(j - 1, k), :],
            peer_send.at[j - 1, k], peer_recv.at[j - 1, k], (cg, ups[j] * 2 + core),
        )

    def own_copy(j, k):
        block = whole.at[spot(vg, k)]
        return rcopy(block, block, own_send.at[j - 1, k], block_recv.at[j - 1, k], (cg, ups[j] * 2 + core))

    def block_wait(j, k):
        block = whole.at[spot(downs[j] * 2 + core, k)]
        rcopy(block, block, own_send.at[j - 1, k], block_recv.at[j - 1, k], pair).wait_recv()

    def pass_copy(h, k):
        block = whole.at[spot(h * 2 + core, k)]
        return rcopy(block, block, pass_send.at[h, k], pair_recv.at[h, k], pair)

    def pass_wait(h, k):
        block = whole.at[spot(h * 2 + 1 - core, k)]
        rcopy(block, block, pass_send.at[h, k], pair_recv.at[h, k], pair).wait_recv()

    for j in list(range(1, n_hi)) + [0]:
        for k in chunks:
            to_core[cut(ups[j], k), :] = part(last_f, ups[j] * 2 + 1 - core, k).astype(BF16)
            core_copy(ups[j], k).start()
    for j in range(1, n_hi):
        for k in chunks:
            core_copy(ups[j], k).wait_recv()
            to_peer[cut(j - 1, k), :] = (
                part(last_f, ups[j] * 2 + core, k) + from_core[cut(ups[j], k), :].astype(F32)
            ).astype(BF16)
            peer_copy(j, k).start()
    column(row_coef_ref, coef)
    for k in chunks:
        core_copy(hi, k).wait_recv()
        messages = part(last_f, vg, k) + from_core[cut(hi, k), :].astype(F32)
        for j in range(1, n_hi):
            peer_copy(j, k).wait_recv()
            messages = messages + from_peer[cut(j - 1, k), :].astype(F32)
        preact = pre[here(k), :] + coef[here(k), :] * messages
        sig = jax.nn.sigmoid(preact)
        grad_pre = cot_ref[here(k), :] * sig * (1.0 + preact * (1.0 - sig))
        whole[spot(vg, k)] = (coef[here(k), :] * grad_pre).astype(BF16)
        for j in range(1, n_hi):
            own_copy(j, k).start()
        pass_copy(hi, k).start()
        update_ref[here(k), :] = con_ref[here(k), :] + preact * sig
        pre[here(k), :] = grad_pre
    local_self[...] = dot(con_ref[...], pre[...], ((0,), (0,)))
    small = Total(n_cg, n_vg, local_self, grad_self_ref, cuts_a, quarters_a, sem_a)
    small.start()
    grad_con_ref[...] = cot_ref[...] + dot(pre[...], self_w_ref[...], ((1,), (1,)))
    column(col_coef_ref, coef)
    for k in chunks:
        for j in range(1, n_hi):
            block_wait(j, k)
            pass_copy(downs[j], k).start()
    for h in range(n_hi):
        for k in chunks:
            pass_wait(h, k)

    tile_step(prev_b, row_ref, whole, ((0,), (0,)))

    def x_copy(zd, k):
        return rcopy(to_x.at[cut(zd, k), :], from_x.at[cut(zd, k), :], x_send.at[zd, k], x_recv.at[zd, k], x_peer)

    def z_copy(zd, way, k):
        step = 1 if way == 0 else -1
        return rcopy(
            to_z.at[cut(zd, k), :], from_z.at[way, cut(zd, k), :],
            z_send.at[way, zd, k], z_recv.at[way, zd, k], ((z + step) * 2 + x, vg),
        )

    def z_arrives(way):
        return z >= 1 if way == 0 else z + 1 < n_z

    order = [(d, way) for d in range(n_z - 1, 0, -1) for way in (0, 1)]

    def place(d, way):
        zd = z + d if way == 0 else z - d
        return zd, (zd >= 0) & (zd < n_z)

    def send_x(zd):
        for k in chunks:
            to_x[cut(zd, k), :] = part(last_b, zd * 2 + 1 - x, k).astype(BF16)
            x_copy(zd, k).start()

    for d, way in order:
        zd, there = place(d, way)
        pl.when(there)(lambda zd=zd: send_x(zd))
    send_x(z)
    small.second()

    for d, way in order:
        zd, there = place(d, way)

        @pl.when(there)
        def _(zd=zd, way=way):
            for k in chunks:
                x_copy(zd, k).wait_recv()
                value = part(last_b, zd * 2 + x, k) + from_x[cut(zd, k), :].astype(F32)

                @pl.when(z_arrives(way))
                def _(k=k, value=value):
                    z_copy(zd, way, k).wait_recv()
                    to_z[cut(zd, k), :] = (value + from_z[way, cut(zd, k), :].astype(F32)).astype(BF16)

                @pl.when(jnp.logical_not(z_arrives(way)))
                def _(k=k, value=value):
                    to_z[cut(zd, k), :] = value.astype(BF16)

                z_copy(zd, way, k).start()

    small.third()
    for k in chunks:
        x_copy(z, k).wait_recv()
        pre[here(k), :] = part(last_b, cg, k) + from_x[cut(z, k), :].astype(F32)
        for way in (0, 1):
            @pl.when(z_arrives(way))
            def _(way=way, k=k):
                z_copy(z, way, k).wait_recv()
                pre[here(k), :] += from_z[way, cut(z, k), :].astype(F32)

        lin = pre[here(k), :] * coef[here(k), :]
        pre[here(k), :] = lin
        term = dot(var_ref[here(k), :], lin, ((0,), (0,)))
        local_msg[...] = term if k == 0 else local_msg[...] + term
    big = Total(n_cg, n_vg, local_msg, grad_msg_ref, cuts_b, quarters_b, sem_b)
    big.start()
    grad_var_ref[...] = dot(pre[...], msg_w_ref[...], ((1,), (1,)))
    big.second()

    for k in chunks:
        for zs in range(n_z):
            gx_copy(zs, k).wait_send()
            x_copy(zs, k).wait_send()
        for d in range(n_z):
            for way in (0, 1):
                zs = z - d if way == 0 else z + d
                on(zs, way, lambda zs=zs, way=way, k=k: gz_copy(zs, way, k).wait_send())
        for d, way in order:
            zd, there = place(d, way)
            pl.when(there)(lambda zd=zd, way=way, k=k: z_copy(zd, way, k).wait_send())
        for h in range(n_hi):
            pass_copy(h, k).wait_send()
            core_copy(h, k).wait_send()
        for j in range(1, n_hi):
            peer_copy(j, k).wait_send()
            own_copy(j, k).wait_send()
    small.finish()
    big.third()
    big.finish()


def chains_kernel(row_blocks, row_ref, col_ref, out_ref):
    count = row_ref.shape[0]
    base = 0
    for index_ref, blocks in ((row_ref, row_blocks), (col_ref, out_ref.shape[0] - 2 * count - row_blocks)):
        last = base + count

        def clear(b, carry):
            out_ref[last + b] = count
            return carry

        lax.fori_loop(0, blocks, clear, 0)
        for k in range(count):
            at = last + index_ref[k]
            out_ref[base + k] = out_ref[at]
            out_ref[at] = k
        base = last + blocks


def chains(row_index, col_index, row_blocks, col_blocks):
    smem = pl.BlockSpec(memory_space=pltpu.SMEM)
    return pl.pallas_call(
        functools.partial(chains_kernel, row_blocks),
        name="chains",
        out_shape=jax.ShapeDtypeStruct((2 * row_index.shape[0] + row_blocks + col_blocks,), jnp.int32),
        in_specs=[smem] * 2,
        out_specs=smem,
    )(row_index, col_index)


def layer(row_index, col_index, patterns, var_embed, msg_weight, col_coef, con_embed, cotangent,
          self_weight, row_coef, time_embed, n_cg, n_vg):
    size = var_embed.shape[0]
    count = patterns.shape[0]
    n_z, n_hi, n_max = n_cg // 2, n_vg // 2, max(n_cg, n_vg)
    others = max(n_hi - 1, 1)
    row_blocks, col_blocks = n_vg * size // TB, n_cg * size // TB
    share = H // n_vg
    vmem, smem, anywhere = (pl.BlockSpec(memory_space=m) for m in (pltpu.VMEM, pltpu.SMEM, pl.ANY))
    full, square = jax.ShapeDtypeStruct((size, H), F32), jax.ShapeDtypeStruct((H, H), F32)
    dma = lambda *n: pltpu.SemaphoreType.DMA(n)
    return pl.pallas_call(
        functools.partial(layer_kernel, n_cg, n_vg),
        name="layer",
        out_shape=(full, full, full, square, square),
        in_specs=[smem, smem, smem, anywhere, vmem, vmem, vmem, anywhere, anywhere, vmem, vmem, vmem],
        out_specs=(vmem,) * 5,
        scratch_shapes=[
            pltpu.VMEM(patterns.shape, BF16),
            pltpu.VMEM((size, H), F32),
            pltpu.VMEM((size, H), F32),
            pltpu.VMEM((size, H), F32),
            pltpu.VMEM((size, H), F32),
            pltpu.VMEM((col_blocks, TB, H), BF16),
            pltpu.VMEM((row_blocks, TB, H), BF16),
            pltpu.VMEM((count + 1, TB, H), F32),
            pltpu.VMEM((n_hi * size, H), BF16),
            pltpu.VMEM((n_hi * size, H), BF16),
            pltpu.VMEM((others * size, H), BF16),
            pltpu.VMEM((others * size, H), BF16),
            pltpu.VMEM((n_z * size, H), BF16),
            pltpu.VMEM((n_z * size, H), BF16),
            pltpu.VMEM((n_z * size, H), BF16),
            pltpu.VMEM((2, n_z * size, H), BF16),
            pltpu.VMEM((H, H), F32),
            pltpu.VMEM((H, H), F32),
            pltpu.VMEM((n_vg - 1, share, H), F32),
            pltpu.VMEM((n_vg - 1, share, H), F32),
            pltpu.VMEM((n_cg, share, H), F32),
            pltpu.VMEM((n_cg, share, H), F32),
            dma(3), dma(2, n_z, CHUNKS), dma(n_z, CHUNKS), dma(n_z, CHUNKS), dma(n_z, CHUNKS),
            dma(n_hi, CHUNKS), dma(n_hi, CHUNKS), dma(others, CHUNKS), dma(others, CHUNKS),
            dma(others, CHUNKS), dma(n_hi, CHUNKS), dma(others, CHUNKS), dma(n_hi, CHUNKS),
            dma(n_z, CHUNKS), dma(n_z, CHUNKS), dma(2, n_z, CHUNKS), dma(2, n_z, CHUNKS),
            dma(6, n_max), dma(6, n_max),
        ],
        compiler_params=pltpu.CompilerParams(
            collective_id=0, has_side_effects=True, vmem_limit_bytes=60000 * 1024
        ),
    )(
        row_index, col_index, chains(row_index, col_index, row_blocks, col_blocks), patterns, var_embed, msg_weight, col_coef.reshape(-1, H),
        con_embed, cotangent, self_weight, row_coef.reshape(-1, H), time_embed.reshape(1, H),
    )


def finish_kernel(*refs):
    half = len(refs) // 2
    for source, target in zip(refs[:half], refs[half:]):
        target[...] = source[...]


def finish(*arrays):
    steps = 2
    specs = [pl.BlockSpec((a.shape[0] // steps, H), lambda i: (i, 0)) for a in arrays]
    return pl.pallas_call(
        finish_kernel,
        name="finish",
        grid=(steps,),
        out_shape=tuple(jax.ShapeDtypeStruct(a.shape, a.dtype) for a in arrays),
        in_specs=specs,
        out_specs=tuple(specs),
    )(*arrays)


def body(
    con_embed, var_embed, row_coef, col_coef, self_weight, msg_weight,
    timestep, tile_rows, tile_cols, pattern, cotangent,
):
    n_cg, n_vg = lax.axis_size("cg"), lax.axis_size("vg")
    frequency = jnp.exp(-math.log(10000.0) * jnp.arange(H // 2, dtype=F32) / (H // 2))
    phases = timestep[0].astype(F32) * frequency
    time_embed = jnp.concatenate([jnp.sin(phases), jnp.cos(phases)])
    return finish(*layer(
        tile_rows.reshape(-1), tile_cols.reshape(-1), pattern.reshape(-1, TB, TB), var_embed, msg_weight,
        col_coef, con_embed, cotangent, self_weight, row_coef, time_embed, n_cg, n_vg,
    ))


def solution(mesh):
    in_specs = (
        P(("cg", "vg"), None),
        P(("vg", "cg"), None),
        P(("cg", "vg")),
        P(("vg", "cg")),
        P(),
        P(),
        P(),
        P("cg", "vg", None),
        P("cg", "vg", None),
        P("cg", "vg", None, None, None),
        P(("cg", "vg"), None),
    )
    out_specs = (P(("cg", "vg"), None), P(("cg", "vg"), None), P(("vg", "cg"), None), P(), P())
    return jax.shard_map(body, mesh=mesh, in_specs=in_specs, out_specs=out_specs, check_vma=False)
```
